32 devices in a mesh: groups: 2 (over y), theta: 16 (over z, x, core).
Axes of the slice: x: 2, y: 2, z: 4, core: 2. Of those that a mesh axis runs over, the one named last changes fastest.
Arguments:
- state_now: float32 [5, 2, 64, 256, 128], P(None, None, 'theta', 'groups'), parts along dimension 3, may hold values from -6 to 6
- state_prev: float32 [5, 2, 64, 256, 128], P(None, None, 'theta', 'groups'), parts along dimension 3, may hold values from -6 to 6
- eddy_visc: float32 [2, 64, 256, 128], P(None, 'theta', 'groups'), parts along dimension 2, may hold values from 0.01 to 0.2
- mean_flow: float32 [2, 4], replicated, may hold values from 0.5 to 1
- offset: int32 [2], P('groups'), parts along dimension 0, may hold values from 0 to 63
Outputs:
- field: float32 [5, 2, 64, 256, 128], P(None, None, 'theta', 'groups'), parts along dimension 3
The draws below stay inside these ranges and needn't reach their ends.
There are 2 independent parts, one for each index of `groups`. The reference program is written for one: setup_inputs(seed, part) draws one part's arguments, and reference() takes and returns one part's arrays. A program takes and returns all parts, laid end to end along the dimension named above; an argument that names none is the same for every part. Nothing has to cross between parts.
All inputs are finite; a program needn't handle non-finite values.
Results may differ from the reference program's by a relative error of at most 0.00002.
Values sent between devices are 32-bit elements; how exact they have to be, the bound alone decides.
A program may use at most 128 MiB of HBM per device.

```python
import math
import jax
import jax.numpy as jnp

R = 128
A = 128
ITERS = 2
NT = 64


def steps_of(key, extent, split, smallest, largest):
    factor_of, own = 1.0, jax.random.fold_in(key, 6)
    for axis_at, shards_of in split:
        steps = jnp.exp(jax.random.uniform(jax.random.fold_in(own, axis_at), (shards_of,), jnp.float32, smallest / len(split), largest / len(split)))
        factor_of = factor_of * jnp.repeat(steps, extent[axis_at] // shards_of).reshape([-1 if axis == axis_at else 1 for axis in range(len(extent))])
    return factor_of


def bell_draw(stream_key, extent, spread, bound, split=(), held_as=jnp.bfloat16):
    level = steps_of(stream_key, extent, split, -0.22, 0.18) if split else 1.0
    entries = jax.random.normal(stream_key, extent, jnp.float32) * spread * level
    return jnp.minimum(jnp.maximum(entries, -bound), bound).astype(held_as)


def setup_inputs(seed: int = 0, part: int = 0) -> dict:
    keys = jax.random.split(jax.random.key(seed), 6)
    part_keys = jax.random.split(jax.random.fold_in(keys[5], part), 6)
    return {
        "state_now": bell_draw(part_keys[0], (5, 2, NT, R, A), 1.0, 6.0, ((2, 16),), jnp.float32),
        "state_prev": bell_draw(part_keys[1], (5, 2, NT, R, A), 1.0, 6.0, ((2, 16),), jnp.float32),
        "eddy_visc": jnp.clip(jnp.exp(math.log(0.2) - 2.9957323 * jax.random.uniform(part_keys[2], (2, NT, R, A), jnp.float32) ** steps_of(part_keys[2], (2, NT, R, A), ((1, 16),), -0.2, 0.2)), 0.01, 0.2),
        "mean_flow": jnp.clip(jax.random.uniform(keys[3], (2, 4), jnp.float32, 0.5, 1.0), 0.5, 1.0),
        "offset": jax.random.randint(part_keys[4], (1,), 0, NT).astype(jnp.int32),
    }


PSEUDO_STEP = 0.2
PHYS_STEP = 1.0
SECTION_WEIGHTS = (0.6, 0.6, 1.0)


def operator_terms(padded, low_ghost, high_ghost, mean_row, eddy_row):
    center = padded[:, 1:-1]
    theta_diff = (padded[:, 2:] - padded[:, :-2]) * 0.5
    neighbours = padded[:, 2:] + padded[:, :-2]
    wall_sign = jnp.array([1.0, 1.0, 1.0, -1.0, 1.0], jnp.float32).reshape(5, 1, 1, 1)
    radial_pad = jnp.concatenate([center[:, :, :1] * wall_sign, center, center[:, :, -1:] * wall_sign], axis=2)
    radial_diff = (radial_pad[:, :, 2:] - radial_pad[:, :, :-2]) * 0.5
    neighbours = neighbours + radial_pad[:, :, 2:] + radial_pad[:, :, :-2]
    axial_pad = jnp.concatenate([low_ghost[..., None], center, high_ghost[..., None]], axis=3)
    axial_diff = (axial_pad[..., 2:] - axial_pad[..., :-2]) * 0.5
    neighbours = neighbours + axial_pad[..., 2:] + axial_pad[..., :-2]
    laplace = neighbours - 6.0 * center
    axial_speed = mean_row[0]
    swirl_speed = mean_row[1]
    density = mean_row[2]
    sound_speed = mean_row[3]
    convect = axial_speed * axial_diff + swirl_speed * theta_diff
    divergence = axial_diff[1] + theta_diff[2] + radial_diff[3]
    pressure_push = jnp.stack([density * divergence, axial_diff[4] / density, theta_diff[4] / density,
                               radial_diff[4] / density, density * sound_speed * sound_speed * divergence])
    return convect + pressure_push - eddy_row * laplace


def wrap_pad(row_field):
    return jnp.concatenate([row_field[:, -1:], row_field, row_field[:, :1]], axis=1)


def reference(state_now, state_prev, eddy_visc, mean_flow, offset):
    shift_cells = offset[0] % NT
    fixed_part = (state_prev - 4.0 * state_now) * (0.5 / PHYS_STEP)
    field = state_now
    for sweep in range(ITERS):
        start_field = field
        for weight in SECTION_WEIGHTS:
            rotor_row = field[:, 0]
            stator_row = field[:, 1]
            rotor_high = jnp.roll(stator_row[..., 0], -shift_cells, axis=1)
            stator_low = jnp.roll(rotor_row[..., -1], shift_cells, axis=1)
            rotor_terms = operator_terms(wrap_pad(rotor_row), jnp.zeros_like(rotor_high), rotor_high,
                                         mean_flow[0], eddy_visc[0])
            stator_terms = operator_terms(wrap_pad(stator_row), stator_low, stator_row[..., -1],
                                          mean_flow[1], eddy_visc[1])
            terms = jnp.stack([rotor_terms, stator_terms], axis=1)
            field = start_field - (weight * PSEUDO_STEP) * (terms + (1.5 / PHYS_STEP) * field + fixed_part)
    return field
```

```python
import functools
import jax
import jax.numpy as jnp
from jax import lax
from jax.experimental import pallas as pl
from jax.experimental.pallas import tpu as pltpu
from jax.sharding import PartitionSpec as P

ITERS = 2
PSEUDO_STEP = 0.2
PHYS_STEP = 1.0
SECTIONS = 3
WEIGHT_EARLY = 0.6
WEIGHT_LAST = 1.0
PAD = 8
CHUNK = 32


def exchange_levels(count):
    levels = []
    stride = 1
    while stride < count:
        radix = 4 if (count // stride) % 4 == 0 else count // stride
        levels.append((stride, radix))
        stride *= radix
    return levels[::-1]


def exchange_messages(count):
    out = []
    for level, (stride, radix) in enumerate(exchange_levels(count)):
        top = radix if stride > 1 else radix + 1
        for j in range(1, top):
            for row in range(2):
                out.append((level, stride * j, row))
    return out


def kernel(
    count, cells, radial,
    scal_ref, digit_ref, now_ref, prev_ref, eddy_ref,
    out_ref,
    fbuf, base, fixed, gcol, ifs, ifr, load_sem, hsend, hrecv, isend, irecv,
):
    me = lax.axis_index("theta")
    levels = exchange_levels(count)
    messages = exchange_messages(count)
    total = ITERS * SECTIONS
    width = fbuf.shape[-1]
    block = ifs.shape[-2]

    def peer(steps):
        return {"theta": lax.rem(me + (steps % count), count)}

    loads = [
        pltpu.make_async_copy(
            now_ref, fbuf.at[0, :, :, pl.ds(1, cells), pl.ds(PAD, radial)], load_sem.at[0]
        ),
        pltpu.make_async_copy(now_ref, base, load_sem.at[1]),
        pltpu.make_async_copy(prev_ref, fixed, load_sem.at[2]),
    ]
    for load in loads:
        load.start()

    reach = {1 % count, count - 1}
    for _, steps, _ in messages:
        reach |= {steps % count, -steps % count}
    reach = sorted(reach - {0})
    barrier = pltpu.get_barrier_semaphore()
    for steps in reach:
        pl.semaphore_signal(
            barrier, inc=1, device_id=peer(steps), device_id_type=pl.DeviceIdType.MESH
        )
    pl.semaphore_wait(barrier, len(reach))

    def halo(slot, row, side):
        source, target = (1, cells + 1) if side == 0 else (cells, 0)
        return pltpu.make_async_remote_copy(
            src_ref=fbuf.at[slot, :, row, source, pl.ds(PAD, radial)],
            dst_ref=fbuf.at[slot, :, row, target, pl.ds(PAD, radial)],
            send_sem=hsend.at[slot, row, side],
            recv_sem=hrecv.at[slot, row, side],
            device_id=peer(-1 if side == 0 else 1),
            device_id_type=pl.DeviceIdType.MESH,
        )

    def plane_message(slot, index):
        level, steps, row = messages[index]
        return pltpu.make_async_remote_copy(
            src_ref=ifs.at[slot, level, row],
            dst_ref=ifr.at[slot, index],
            send_sem=isend.at[slot, index],
            recv_sem=irecv.at[slot, index],
            device_id=peer(steps if row == 0 else -steps),
            device_id_type=pl.DeviceIdType.MESH,
        )

    def of_level(level):
        return [index for index, message in enumerate(messages) if message[0] == level]

    def ghosts(slot, row, t):
        for c in range(5):
            sign = -1.0 if c == 3 else 1.0
            fbuf[slot, c, row, t, pl.ds(PAD - 1, 1), :] = (
                sign * fbuf[slot, c, row, t, pl.ds(PAD, 1), :]
            )
            fbuf[slot, c, row, t, pl.ds(PAD + radial, 1), :] = (
                sign * fbuf[slot, c, row, t, pl.ds(PAD + radial - 1, 1), :]
            )

    lane = lax.broadcasted_iota(jnp.int32, (radial, width), 1)

    def pack(slot):
        acc = jnp.zeros((radial, width), jnp.float32)
        for row in range(2):
            edge = width - 1 if row == 0 else 0
            for t in range(cells):
                for c in range(5):
                    j = row * block + t * 5 + c
                    plane = fbuf[slot, c, row, t + 1, pl.ds(PAD, radial), :]
                    acc = jnp.where(lane == j, pltpu.roll(plane, (j - edge) % width, 1), acc)
        turned = acc.T
        for row in range(2):
            ifs[slot, 0, row] = turned[row * block : (row + 1) * block]

    def publish(slot):
        pack(slot)
        for index in of_level(0):
            plane_message(slot, index).start()
        for row in range(2):
            for side in range(2):
                halo(slot, row, side).start()

    def pick(values, digit):
        out = values[0]
        for j in range(1, len(values)):
            out = jnp.where(digit == j, values[j], out)
        return out

    def interface(slot):
        near = far = None
        for level, (stride, radix) in enumerate(levels):
            got = ([ifs[slot, level, 0]], [ifs[slot, level, 1]])
            for index in of_level(level):
                plane_message(slot, index).wait()
            for index in of_level(level):
                got[messages[index][2]].append(ifr[slot, index])
            digit = digit_ref[level]
            near = [pick(got[row][:radix], digit) for row in range(2)]
            if stride > 1:
                for row in range(2):
                    ifs[slot, level + 1, row] = near[row]
                for index in of_level(level + 1):
                    plane_message(slot, index).start()
            else:
                far = [pick(got[row][1 : radix + 1], digit) for row in range(2)]
        used = 5 * cells
        within = digit_ref[len(levels)]
        from_rotor = jnp.concatenate([far[0][:used], near[0][:used]], axis=0)
        from_stator = jnp.concatenate([near[1][:used], far[1][:used]], axis=0)
        low = pick(
            [from_rotor[5 * (cells - m) : 5 * (2 * cells - m)] for m in range(cells)], within
        )
        high = pick([from_stator[5 * m : 5 * (m + cells)] for m in range(cells)], within)
        gap = jnp.zeros((block - used, width), jnp.float32)
        rest = jnp.zeros((width - 2 * block, width), jnp.float32)
        gcol[...] = jnp.concatenate([high, gap, low, gap, rest], axis=0).T

    small = lax.broadcasted_iota(jnp.int32, (CHUNK, width), 1)
    is_first = small == 0
    is_last = small == width - 1

    def layer(slot, new, row, t, k):
        half_u = scal_ref[row, 0] * (0.5 * k)
        half_v = scal_ref[row, 1] * (0.5 * k)
        push_rho = scal_ref[row, 2] * (0.5 * k)
        push_inv = scal_ref[row, 3] * (0.5 * k)
        push_p = scal_ref[row, 4] * (0.5 * k)

        def body(i, carry):
            r0 = pl.multiple_of(i * CHUNK, CHUNK)
            ke = eddy_ref[row, t - 1, pl.ds(r0, CHUNK), :] * k
            cf = ke * 6.0 + (1.5 / PHYS_STEP) * k
            columns = gcol[pl.ds(r0, CHUNK), :]
            partial = []
            extra = {}
            div = None
            for c in range(5):
                f = fbuf[slot, c, row, t, pl.ds(r0 + PAD, CHUNK), :]
                rm = fbuf[slot, c, row, t, pl.ds(r0 + (PAD - 1), CHUNK), :]
                rp = fbuf[slot, c, row, t, pl.ds(r0 + (PAD + 1), CHUNK), :]
                tm = fbuf[slot, c, row, t - 1, pl.ds(r0 + PAD, CHUNK), :]
                tp = fbuf[slot, c, row, t + 1, pl.ds(r0 + PAD, CHUNK), :]
                am = pltpu.roll(f, 1, 1)
                ap = pltpu.roll(f, width - 1, 1)
                j = row * block + (t - 1) * 5 + c
                if row == 0:
                    am = jnp.where(is_first, 0.0, am)
                    ap = jnp.where(is_last, pltpu.roll(columns, width - 1 - j, 1), ap)
                else:
                    am = jnp.where(
                        is_first, pltpu.roll(columns, (width - j) % width, 1), am
                    )
                    ap = jnp.where(is_last, f, ap)
                da = ap - am
                dt = tp - tm
                around = (ap + am) + (tp + tm) + (rp + rm)
                value = (
                    base[c, row, t - 1, pl.ds(r0, CHUNK), :]
                    - k * fixed[c, row, t - 1, pl.ds(r0, CHUNK), :]
                    - cf * f
                    + ke * around
                    - half_u * da
                    - half_v * dt
                )
                if c == 1:
                    div = da
                elif c == 2:
                    div = div + dt
                elif c == 3:
                    div = div + (rp - rm)
                elif c == 4:
                    extra = {1: da, 2: dt, 3: rp - rm}
                partial.append(value)
            for c in range(5):
                if c == 0:
                    value = partial[0] - push_rho * div
                elif c == 4:
                    value = partial[4] - push_p * div
                else:
                    value = partial[c] - push_inv * extra[c]
                fbuf[new, c, row, t, pl.ds(r0 + PAD, CHUNK), :] = value
            return carry

        lax.fori_loop(0, radial // CHUNK, body, 0)
        ghosts(new, row, t)

    for load in loads:
        load.wait()
    for row in range(2):
        for t in range(cells):
            ghosts(0, row, t + 1)
    publish(0)

    def prepare(t, carry):
        for c in range(5):
            for row in range(2):
                fixed[c, row, t] = (0.5 / PHYS_STEP) * fixed[c, row, t] - (
                    2.0 / PHYS_STEP
                ) * base[c, row, t]
        return carry

    lax.fori_loop(0, cells, prepare, 0)

    def section(s, carry):
        slot = lax.rem(s, 2)
        new = 1 - slot
        k = jnp.where(
            lax.rem(s, SECTIONS) == SECTIONS - 1,
            jnp.float32(WEIGHT_LAST * PSEUDO_STEP),
            jnp.float32(WEIGHT_EARLY * PSEUDO_STEP),
        )

        @pl.when(jnp.logical_and(s > 0, lax.rem(s, SECTIONS) == 0))
        def _():
            def keep(t, carry):
                for c in range(5):
                    for row in range(2):
                        base[c, row, t] = fbuf[slot, c, row, t + 1, pl.ds(PAD, radial), :]
                return carry

            lax.fori_loop(0, cells, keep, 0)

        interface(slot)
        for row in range(2):
            for t in range(2, cells):
                layer(slot, new, row, t, k)

        @pl.when(s > 0)
        def _():
            for row in range(2):
                for side in range(2):
                    halo(new, row, side).wait_send()

        for row in range(2):
            halo(slot, row, 1).wait_recv()
            if cells == 1:
                halo(slot, row, 0).wait_recv()
            layer(slot, new, row, 1, k)
            if cells > 1:
                halo(slot, row, 0).wait_recv()
                layer(slot, new, row, cells, k)

        @pl.when(s < total - 1)
        def _():
            publish(new)

        return carry

    lax.fori_loop(0, total, section, 0)
    for row in range(2):
        for side in range(2):
            halo((total - 1) % 2, row, side).wait_send()
    store = pltpu.make_async_copy(
        fbuf.at[total % 2, :, :, pl.ds(1, cells), pl.ds(PAD, radial)], out_ref, load_sem.at[0]
    )
    store.start()
    store.wait()


def per_device(state_now, state_prev, eddy_visc, mean_flow, offset):
    _, _, cells, radial, width = state_now.shape
    count = lax.axis_size("theta")
    levels = exchange_levels(count)
    messages = exchange_messages(count)
    shift_cells = offset[0] % (cells * count)
    sectors = shift_cells // cells
    digits = jnp.stack(
        [sectors // stride % radix for stride, radix in levels] + [shift_cells % cells]
    ).astype(jnp.int32)
    scalars = jnp.stack(
        [
            mean_flow[:, 0],
            mean_flow[:, 1],
            mean_flow[:, 2],
            1.0 / mean_flow[:, 2],
            mean_flow[:, 2] * mean_flow[:, 3] * mean_flow[:, 3],
        ],
        axis=1,
    )
    block = -(-5 * cells // 8) * 8
    f32 = jnp.float32
    return pl.pallas_call(
        functools.partial(kernel, count, cells, radial),
        out_shape=jax.ShapeDtypeStruct(state_now.shape, f32),
        in_specs=[
            pl.BlockSpec(memory_space=pltpu.SMEM),
            pl.BlockSpec(memory_space=pltpu.SMEM),
            pl.BlockSpec(memory_space=pl.ANY),
            pl.BlockSpec(memory_space=pl.ANY),
            pl.BlockSpec(memory_space=pltpu.VMEM),
        ],
        out_specs=pl.BlockSpec(memory_space=pl.ANY),
        scratch_shapes=[
            pltpu.VMEM((2, 5, 2, cells + 2, radial + 2 * PAD, width), f32),
            pltpu.VMEM((5, 2, cells, radial, width), f32),
            pltpu.VMEM((5, 2, cells, radial, width), f32),
            pltpu.VMEM((radial, width), f32),
            pltpu.VMEM((2, len(levels), 2, block, radial), f32),
            pltpu.VMEM((2, len(messages), block, radial), f32),
            pltpu.SemaphoreType.DMA((3,)),
            pltpu.SemaphoreType.DMA((2, 2, 2)),
            pltpu.SemaphoreType.DMA((2, 2, 2)),
            pltpu.SemaphoreType.DMA((2, len(messages))),
            pltpu.SemaphoreType.DMA((2, len(messages))),
        ],
        compiler_params=pltpu.CompilerParams(
            collective_id=0, has_side_effects=True, vmem_limit_bytes=48 * 1024 * 1024
        ),
    )(scalars, digits, state_now, state_prev, eddy_visc)


def solution(mesh):
    placed = (
        P(None, None, "theta", "groups", None),
        P(None, None, "theta", "groups", None),
        P(None, "theta", "groups", None),
        P(),
        P("groups"),
    )
    return jax.shard_map(
        per_device,
        mesh=mesh,
        in_specs=placed,
        out_specs=P(None, None, "theta", "groups", None),
        check_vma=False,
    )
```

```python
import functools
import jax
import jax.numpy as jnp
from jax import lax
from jax.experimental import pallas as pl
from jax.experimental.pallas import tpu as pltpu
from jax.sharding import PartitionSpec as P

ITERS = 2
PSEUDO_STEP = 0.2
PHYS_STEP = 1.0
SECTIONS = 3
WEIGHT_EARLY = 0.6
WEIGHT_LAST = 1.0
PAD = 8
CHUNK = 64


def exchange_levels(count):
    levels = []
    stride = 1
    while stride < count:
        radix = 4 if (count // stride) % 4 == 0 else count // stride
        levels.append((stride, radix))
        stride *= radix
    return levels[::-1]


def exchange_messages(count):
    out = []
    for level, (stride, radix) in enumerate(exchange_levels(count)):
        top = radix if stride > 1 else radix + 1
        for j in range(1, top):
            for row in range(2):
                out.append((level, stride * j, row))
    return out


def kernel(
    count, cells, radial,
    scal_ref, digit_ref, now_ref, prev_ref, eddy_ref,
    out_ref,
    fbuf, base, fixed, gcol, packed, ifs, ifr, load_sem, hsend, hrecv, isend, irecv,
):
    me = lax.axis_index("theta")
    levels = exchange_levels(count)
    messages = exchange_messages(count)
    total = ITERS * SECTIONS
    width = fbuf.shape[-1]
    block = ifs.shape[-2]

    def peer(steps):
        return {"theta": lax.rem(me + (steps % count), count)}

    loads = [
        pltpu.make_async_copy(
            now_ref, fbuf.at[0, :, :, pl.ds(1, cells), pl.ds(PAD, radial)], load_sem.at[0]
        ),
        pltpu.make_async_copy(now_ref, base, load_sem.at[1]),
        pltpu.make_async_copy(prev_ref, fixed, load_sem.at[2]),
    ]
    for load in loads:
        load.start()

    reach = {1 % count, count - 1}
    for _, steps, _ in messages:
        reach |= {steps % count, -steps % count}
    reach = sorted(reach - {0})
    barrier = pltpu.get_barrier_semaphore()
    for steps in reach:
        pl.semaphore_signal(
            barrier, inc=1, device_id=peer(steps), device_id_type=pl.DeviceIdType.MESH
        )
    pl.semaphore_wait(barrier, len(reach))

    def halo(slot, row, side):
        source, target = (1, cells + 1) if side == 0 else (cells, 0)
        return pltpu.make_async_remote_copy(
            src_ref=fbuf.at[slot, :, row, source, pl.ds(PAD, radial)],
            dst_ref=fbuf.at[slot, :, row, target, pl.ds(PAD, radial)],
            send_sem=hsend.at[slot, row, side],
            recv_sem=hrecv.at[slot, row, side],
            device_id=peer(-1 if side == 0 else 1),
            device_id_type=pl.DeviceIdType.MESH,
        )

    def plane_message(slot, index):
        level, steps, row = messages[index]
        return pltpu.make_async_remote_copy(
            src_ref=ifs.at[slot, level, row],
            dst_ref=ifr.at[slot, index],
            send_sem=isend.at[slot, index],
            recv_sem=irecv.at[slot, index],
            device_id=peer(steps if row == 0 else -steps),
            device_id_type=pl.DeviceIdType.MESH,
        )

    def of_level(level):
        return [index for index, message in enumerate(messages) if message[0] == level]

    def ghosts(slot, row, t):
        for c in range(5):
            sign = -1.0 if c == 3 else 1.0
            fbuf[slot, c, row, t, pl.ds(PAD - 1, 1), :] = (
                sign * fbuf[slot, c, row, t, pl.ds(PAD, 1), :]
            )
            fbuf[slot, c, row, t, pl.ds(PAD + radial, 1), :] = (
                sign * fbuf[slot, c, row, t, pl.ds(PAD + radial - 1, 1), :]
            )

    lane = lax.broadcasted_iota(jnp.int32, (radial, width), 1)

    def pack(slot, row, layers, fresh):
        acc = jnp.zeros((radial, width), jnp.float32) if fresh else packed[row]
        edge = width - 1 if row == 0 else 0
        for t in layers:
            for c in range(5):
                j = (t - 1) * 5 + c
                plane = fbuf[slot, c, row, t, pl.ds(PAD, radial), :]
                acc = jnp.where(lane == j, pltpu.roll(plane, (j - edge) % width, 1), acc)
        packed[row] = acc

    def send_plane(slot, row):
        ifs[slot, 0, row] = packed[row].T[:block]
        for index in of_level(0):
            if messages[index][2] == row:
                plane_message(slot, index).start()

    def send_halo(slot, row):
        for side in range(2):
            halo(slot, row, side).start()

    def pick(values, digit):
        out = values[0]
        for j in range(1, len(values)):
            out = jnp.where(digit == j, values[j], out)
        return out

    def interface(slot):
        near = far = None
        for level, (stride, radix) in enumerate(levels):
            got = ([ifs[slot, level, 0]], [ifs[slot, level, 1]])
            for index in of_level(level):
                plane_message(slot, index).wait()
            for index in of_level(level):
                got[messages[index][2]].append(ifr[slot, index])
            digit = digit_ref[level]
            near = [pick(got[row][:radix], digit) for row in range(2)]
            if stride > 1:
                for row in range(2):
                    ifs[slot, level + 1, row] = near[row]
                for index in of_level(level + 1):
                    plane_message(slot, index).start()
            if level == max(0, len(levels) - 2):
                send_halo(slot, 1)
            else:
                far = [pick(got[row][1 : radix + 1], digit) for row in range(2)]
        used = 5 * cells
        within = digit_ref[len(levels)]
        from_rotor = jnp.concatenate([far[0][:used], near[0][:used]], axis=0)
        from_stator = jnp.concatenate([near[1][:used], far[1][:used]], axis=0)
        low = pick(
            [from_rotor[5 * (cells - m) : 5 * (2 * cells - m)] for m in range(cells)], within
        )
        high = pick([from_stator[5 * m : 5 * (m + cells)] for m in range(cells)], within)
        gap = jnp.zeros((block - used, width), jnp.float32)
        rest = jnp.zeros((width - 2 * block, width), jnp.float32)
        gcol[...] = jnp.concatenate([high, gap, low, gap, rest], axis=0).T

    small = lax.broadcasted_iota(jnp.int32, (CHUNK, width), 1)
    is_first = small == 0
    is_last = small == width - 1

    def layer(slot, new, row, t, k, ghosted):
        half_u = scal_ref[row, 0] * (0.5 * k)
        half_v = scal_ref[row, 1] * (0.5 * k)
        push_rho = scal_ref[row, 2] * (0.5 * k)
        push_inv = scal_ref[row, 3] * (0.5 * k)
        push_p = scal_ref[row, 4] * (0.5 * k)

        def body(i, carry):
            r0 = pl.multiple_of(i * CHUNK, CHUNK)
            ke = eddy_ref[row, t - 1, pl.ds(r0, CHUNK), :] * k
            cf = ke * 6.0 + (1.5 / PHYS_STEP) * k
            columns = gcol[pl.ds(r0, CHUNK), :] if ghosted else None
            partial = []
            extra = {}
            div = None
            for c in range(5):
                f = fbuf[slot, c, row, t, pl.ds(r0 + PAD, CHUNK), :]
                rm = fbuf[slot, c, row, t, pl.ds(r0 + (PAD - 1), CHUNK), :]
                rp = fbuf[slot, c, row, t, pl.ds(r0 + (PAD + 1), CHUNK), :]
                tm = fbuf[slot, c, row, t - 1, pl.ds(r0 + PAD, CHUNK), :]
                tp = fbuf[slot, c, row, t + 1, pl.ds(r0 + PAD, CHUNK), :]
                am = pltpu.roll(f, 1, 1)
                ap = pltpu.roll(f, width - 1, 1)
                j = row * block + (t - 1) * 5 + c
                if row == 0:
                    am = jnp.where(is_first, 0.0, am)
                    ghost = pltpu.roll(columns, width - 1 - j, 1) if ghosted else 0.0
                    ap = jnp.where(is_last, ghost, ap)
                else:
                    ghost = pltpu.roll(columns, (width - j) % width, 1) if ghosted else 0.0
                    am = jnp.where(is_first, ghost, am)
                    ap = jnp.where(is_last, f, ap)
                da = ap - am
                dt = tp - tm
                around = (ap + am) + (tp + tm) + (rp + rm)
                value = (
                    base[c, row, t - 1, pl.ds(r0, CHUNK), :]
                    - k * fixed[c, row, t - 1, pl.ds(r0, CHUNK), :]
                    - cf * f
                    + ke * around
                    - half_u * da
                    - half_v * dt
                )
                if c == 1:
                    div = da
                elif c == 2:
                    div = div + dt
                elif c == 3:
                    div = div + (rp - rm)
                elif c == 4:
                    extra = {1: da, 2: dt, 3: rp - rm}
                partial.append(value)
            for c in range(5):
                if c == 0:
                    value = partial[0] - push_rho * div
                elif c == 4:
                    value = partial[4] - push_p * div
                else:
                    value = partial[c] - push_inv * extra[c]
                fbuf[new, c, row, t, pl.ds(r0 + PAD, CHUNK), :] = value
            return carry

        lax.fori_loop(0, radial // CHUNK, body, 0)
        if ghosted:
            ghosts(new, row, t)

    def patch(new, row, t, k):
        sign = 1.0 if row == 0 else -1.0
        half_u = scal_ref[row, 0] * (0.5 * sign * k)
        push_rho = scal_ref[row, 2] * (0.5 * sign * k)
        push_inv = scal_ref[row, 3] * (0.5 * sign * k)
        push_p = scal_ref[row, 4] * (0.5 * sign * k)
        here = is_last if row == 0 else is_first
        edge = width - 1 if row == 0 else 0

        def body(i, carry):
            r0 = pl.multiple_of(i * CHUNK, CHUNK)
            scale = eddy_ref[row, t - 1, pl.ds(r0, CHUNK), :] * k - half_u
            columns = gcol[pl.ds(r0, CHUNK), :]
            ghost = []
            for c in range(5):
                j = row * block + (t - 1) * 5 + c
                ghost.append(jnp.where(here, pltpu.roll(columns, (edge - j) % width, 1), 0.0))
            for c in range(5):
                delta = scale * ghost[c]
                if c == 0:
                    delta = delta - push_rho * ghost[1]
                elif c == 1:
                    delta = delta - push_inv * ghost[4]
                elif c == 4:
                    delta = delta - push_p * ghost[1]
                where = (new, c, row, t, pl.ds(r0 + PAD, CHUNK))
                fbuf[where] = fbuf[where] + delta
            return carry

        lax.fori_loop(0, radial // CHUNK, body, 0)
        ghosts(new, row, t)

    for load in loads:
        load.wait()
    for row in range(2):
        for t in range(cells):
            ghosts(0, row, t + 1)
    for row in range(2):
        pack(0, row, range(1, cells + 1), True)
        send_plane(0, row)
    send_halo(0, 0)

    def prepare(t, carry):
        for c in range(5):
            for row in range(2):
                fixed[c, row, t] = (0.5 / PHYS_STEP) * fixed[c, row, t] - (
                    2.0 / PHYS_STEP
                ) * base[c, row, t]
        return carry

    lax.fori_loop(0, cells, prepare, 0)

    def section(s, carry):
        slot = lax.rem(s, 2)
        new = 1 - slot
        k = jnp.where(
            lax.rem(s, SECTIONS) == SECTIONS - 1,
            jnp.float32(WEIGHT_LAST * PSEUDO_STEP),
            jnp.float32(WEIGHT_EARLY * PSEUDO_STEP),
        )

        @pl.when(jnp.logical_and(s > 0, lax.rem(s, SECTIONS) == 0))
        def _():
            def keep(t, carry):
                for c in range(5):
                    for row in range(2):
                        base[c, row, t] = fbuf[slot, c, row, t + 1, pl.ds(PAD, radial), :]
                return carry

            lax.fori_loop(0, cells, keep, 0)

        inner = range(2, cells)
        for row in range(2):
            for t in inner:
                layer(slot, new, row, t, k, False)
        interface(slot)
        for row in range(2):
            for t in inner:
                patch(new, row, t, k)
            pack(new, row, inner, True)

        @pl.when(s > 0)
        def _():
            for row in range(2):
                for side in range(2):
                    halo(new, row, side).wait_send()

        for row in range(2):
            halo(slot, row, 1).wait_recv()
            if cells == 1:
                halo(slot, row, 0).wait_recv()
            layer(slot, new, row, 1, k, True)
            if cells > 1:
                halo(slot, row, 0).wait_recv()
                layer(slot, new, row, cells, k, True)

            @pl.when(s < total - 1)
            def _():
                pack(new, row, sorted({1, cells}), False)
                send_plane(new, row)
                if row == 0:
                    send_halo(new, 0)

        return carry

    lax.fori_loop(0, total, section, 0)
    for row in range(2):
        for side in range(2):
            halo((total - 1) % 2, row, side).wait_send()
    store = pltpu.make_async_copy(
        fbuf.at[total % 2, :, :, pl.ds(1, cells), pl.ds(PAD, radial)], out_ref, load_sem.at[0]
    )
    store.start()
    store.wait()


def per_device(state_now, state_prev, eddy_visc, mean_flow, offset):
    _, _, cells, radial, width = state_now.shape
    count = lax.axis_size("theta")
    levels = exchange_levels(count)
    messages = exchange_messages(count)
    shift_cells = offset[0] % (cells * count)
    sectors = shift_cells // cells
    digits = jnp.stack(
        [sectors // stride % radix for stride, radix in levels] + [shift_cells % cells]
    ).astype(jnp.int32)
    scalars = jnp.stack(
        [
            mean_flow[:, 0],
            mean_flow[:, 1],
            mean_flow[:, 2],
            1.0 / mean_flow[:, 2],
            mean_flow[:, 2] * mean_flow[:, 3] * mean_flow[:, 3],
        ],
        axis=1,
    )
    block = -(-5 * cells // 8) * 8
    f32 = jnp.float32
    return pl.pallas_call(
        functools.partial(kernel, count, cells, radial),
        out_shape=jax.ShapeDtypeStruct(state_now.shape, f32),
        in_specs=[
            pl.BlockSpec(memory_space=pltpu.SMEM),
            pl.BlockSpec(memory_space=pltpu.SMEM),
            pl.BlockSpec(memory_space=pl.ANY),
            pl.BlockSpec(memory_space=pl.ANY),
            pl.BlockSpec(memory_space=pltpu.VMEM),
        ],
        out_specs=pl.BlockSpec(memory_space=pl.ANY),
        scratch_shapes=[
            pltpu.VMEM((2, 5, 2, cells + 2, radial + 2 * PAD, width), f32),
            pltpu.VMEM((5, 2, cells, radial, width), f32),
            pltpu.VMEM((5, 2, cells, radial, width), f32),
            pltpu.VMEM((radial, width), f32),
            pltpu.VMEM((2, radial, width), f32),
            pltpu.VMEM((2, len(levels), 2, block, radial), f32),
            pltpu.VMEM((2, len(messages), block, radial), f32),
            pltpu.SemaphoreType.DMA((3,)),
            pltpu.SemaphoreType.DMA((2, 2, 2)),
            pltpu.SemaphoreType.DMA((2, 2, 2)),
            pltpu.SemaphoreType.DMA((2, len(messages))),
            pltpu.SemaphoreType.DMA((2, len(messages))),
        ],
        compiler_params=pltpu.CompilerParams(
            collective_id=0, has_side_effects=True, vmem_limit_bytes=48 * 1024 * 1024
        ),
    )(scalars, digits, state_now, state_prev, eddy_visc)


def solution(mesh):
    placed = (
        P(None, None, "theta", "groups", None),
        P(None, None, "theta", "groups", None),
        P(None, "theta", "groups", None),
        P(),
        P("groups"),
    )
    return jax.shard_map(
        per_device,
        mesh=mesh,
        in_specs=placed,
        out_specs=P(None, None, "theta", "groups", None),
        check_vma=False,
    )
```

```python
import functools
import jax
import jax.numpy as jnp
from jax import lax
from jax.experimental import pallas as pl
from jax.experimental.pallas import tpu as pltpu
from jax.sharding import PartitionSpec as P

ITERS = 2
PSEUDO_STEP = 0.2
PHYS_STEP = 1.0
SECTIONS = 3
WEIGHT_EARLY = 0.6
WEIGHT_LAST = 1.0
PAD = 8
CHUNK = 64
FIRST = (2, 1)


def exchange_levels(count):
    levels = []
    stride = 1
    while stride < count:
        radix = 4 if (count // stride) % 4 == 0 else count // stride
        levels.append((stride, radix))
        stride *= radix
    return levels[::-1]


def exchange_messages(count):
    out = []
    for level, (stride, radix) in enumerate(exchange_levels(count)):
        top = radix if stride > 1 else radix + 1
        for j in range(1, top):
            for row in range(2):
                out.append((level, stride * j, row))
    return out


def kernel(
    count, cells, radial,
    scal_ref, digit_ref, now_ref, prev_ref, eddy_ref,
    out_ref,
    fbuf, base, fixed, gcol, packed, ifs, ifr, load_sem, hsend, hrecv, isend, irecv,
):
    me = lax.axis_index("theta")
    levels = exchange_levels(count)
    messages = exchange_messages(count)
    total = ITERS * SECTIONS
    width = fbuf.shape[-1]
    block = ifs.shape[-2]

    def peer(steps):
        return {"theta": lax.rem(me + (steps % count), count)}

    loads = [
        pltpu.make_async_copy(
            now_ref, fbuf.at[0, :, :, pl.ds(1, cells), pl.ds(PAD, radial)], load_sem.at[0]
        ),
        pltpu.make_async_copy(now_ref, base, load_sem.at[1]),
        pltpu.make_async_copy(prev_ref, fixed, load_sem.at[2]),
    ]
    for load in loads:
        load.start()

    reach = {1 % count, count - 1}
    for _, steps, _ in messages:
        reach |= {steps % count, -steps % count}
    reach = sorted(reach - {0})
    barrier = pltpu.get_barrier_semaphore()
    for steps in reach:
        pl.semaphore_signal(
            barrier, inc=1, device_id=peer(steps), device_id_type=pl.DeviceIdType.MESH
        )
    pl.semaphore_wait(barrier, len(reach))

    def halo(slot, row, side, piece=0):
        part = pl.ds(0, FIRST[row]) if piece == 0 else pl.ds(FIRST[row], 5 - FIRST[row])
        source, target = (1, cells + 1) if side == 0 else (cells, 0)
        return pltpu.make_async_remote_copy(
            src_ref=fbuf.at[slot, part, row, source, pl.ds(PAD, radial)],
            dst_ref=fbuf.at[slot, part, row, target, pl.ds(PAD, radial)],
            send_sem=hsend.at[slot, row, side, piece],
            recv_sem=hrecv.at[slot, row, side, piece],
            device_id=peer(-1 if side == 0 else 1),
            device_id_type=pl.DeviceIdType.MESH,
        )

    def plane_message(slot, index):
        level, steps, row = messages[index]
        return pltpu.make_async_remote_copy(
            src_ref=ifs.at[slot, level, row],
            dst_ref=ifr.at[slot, index],
            send_sem=isend.at[slot, index],
            recv_sem=irecv.at[slot, index],
            device_id=peer(steps if row == 0 else -steps),
            device_id_type=pl.DeviceIdType.MESH,
        )

    def of_level(level):
        return [index for index, message in enumerate(messages) if message[0] == level]

    def ghosts(slot, row, t):
        for c in range(5):
            sign = -1.0 if c == 3 else 1.0
            fbuf[slot, c, row, t, pl.ds(PAD - 1, 1), :] = (
                sign * fbuf[slot, c, row, t, pl.ds(PAD, 1), :]
            )
            fbuf[slot, c, row, t, pl.ds(PAD + radial, 1), :] = (
                sign * fbuf[slot, c, row, t, pl.ds(PAD + radial - 1, 1), :]
            )

    lane = lax.broadcasted_iota(jnp.int32, (radial, width), 1)

    def pack(slot, row, layers, fresh):
        acc = jnp.zeros((radial, width), jnp.float32) if fresh else packed[row]
        edge = width - 1 if row == 0 else 0
        for t in layers:
            for c in range(5):
                j = (t - 1) * 5 + c
                plane = fbuf[slot, c, row, t, pl.ds(PAD, radial), :]
                acc = jnp.where(lane == j, pltpu.roll(plane, (j - edge) % width, 1), acc)
        packed[row] = acc

    def send_plane(slot, row):
        ifs[slot, 0, row] = packed[row].T[:block]
        for index in of_level(0):
            if messages[index][2] == row:
                plane_message(slot, index).start()

    def send_halo(slot, row, pieces=(0, 1)):
        for piece in pieces:
            for side in range(2):
                halo(slot, row, side, piece).start()

    def halo_wait_send(slot, row, side):
        for piece in range(2):
            halo(slot, row, side, piece).wait_send()

    def halo_wait_recv(slot, row, side):
        for piece in range(2):
            halo(slot, row, side, piece).wait_recv()

    def pick(values, digit):
        out = values[0]
        for j in range(1, len(values)):
            out = jnp.where(digit == j, values[j], out)
        return out

    def interface(slot):
        near = far = None
        for level, (stride, radix) in enumerate(levels):
            got = ([ifs[slot, level, 0]], [ifs[slot, level, 1]])
            for index in of_level(level):
                plane_message(slot, index).wait()
            for index in of_level(level):
                got[messages[index][2]].append(ifr[slot, index])
            digit = digit_ref[level]
            near = [pick(got[row][:radix], digit) for row in range(2)]
            if stride > 1:
                for row in range(2):
                    ifs[slot, level + 1, row] = near[row]
                for index in of_level(level + 1):
                    plane_message(slot, index).start()
            if level == max(0, len(levels) - 2):
                send_halo(slot, 1, (1,))
            else:
                far = [pick(got[row][1 : radix + 1], digit) for row in range(2)]
        used = 5 * cells
        within = digit_ref[len(levels)]
        from_rotor = jnp.concatenate([far[0][:used], near[0][:used]], axis=0)
        from_stator = jnp.concatenate([near[1][:used], far[1][:used]], axis=0)
        low = pick(
            [from_rotor[5 * (cells - m) : 5 * (2 * cells - m)] for m in range(cells)], within
        )
        high = pick([from_stator[5 * m : 5 * (m + cells)] for m in range(cells)], within)
        gap = jnp.zeros((block - used, width), jnp.float32)
        rest = jnp.zeros((width - 2 * block, width), jnp.float32)
        gcol[...] = jnp.concatenate([high, gap, low, gap, rest], axis=0).T

    small = lax.broadcasted_iota(jnp.int32, (CHUNK, width), 1)
    is_first = small == 0
    is_last = small == width - 1

    def layer(slot, new, row, t, k, ghosted):
        half_u = scal_ref[row, 0] * (0.5 * k)
        half_v = scal_ref[row, 1] * (0.5 * k)
        push_rho = scal_ref[row, 2] * (0.5 * k)
        push_inv = scal_ref[row, 3] * (0.5 * k)
        push_p = scal_ref[row, 4] * (0.5 * k)

        def body(i, carry):
            r0 = pl.multiple_of(i * CHUNK, CHUNK)
            ke = eddy_ref[row, t - 1, pl.ds(r0, CHUNK), :] * k
            cf = ke * 6.0 + (1.5 / PHYS_STEP) * k
            columns = gcol[pl.ds(r0, CHUNK), :] if ghosted else None
            partial = []
            extra = {}
            div = None
            for c in range(5):
                f = fbuf[slot, c, row, t, pl.ds(r0 + PAD, CHUNK), :]
                rm = fbuf[slot, c, row, t, pl.ds(r0 + (PAD - 1), CHUNK), :]
                rp = fbuf[slot, c, row, t, pl.ds(r0 + (PAD + 1), CHUNK), :]
                tm = fbuf[slot, c, row, t - 1, pl.ds(r0 + PAD, CHUNK), :]
                tp = fbuf[slot, c, row, t + 1, pl.ds(r0 + PAD, CHUNK), :]
                am = pltpu.roll(f, 1, 1)
                ap = pltpu.roll(f, width - 1, 1)
                j = row * block + (t - 1) * 5 + c
                if row == 0:
                    am = jnp.where(is_first, 0.0, am)
                    ghost = pltpu.roll(columns, width - 1 - j, 1) if ghosted else 0.0
                    ap = jnp.where(is_last, ghost, ap)
                else:
                    ghost = pltpu.roll(columns, (width - j) % width, 1) if ghosted else 0.0
                    am = jnp.where(is_first, ghost, am)
                    ap = jnp.where(is_last, f, ap)
                da = ap - am
                dt = tp - tm
                around = (ap + am) + (tp + tm) + (rp + rm)
                value = (
                    base[c, row, t - 1, pl.ds(r0, CHUNK), :]
                    - k * fixed[c, row, t - 1, pl.ds(r0, CHUNK), :]
                    - cf * f
                    + ke * around
                    - half_u * da
                    - half_v * dt
                )
                if c == 1:
                    div = da
                elif c == 2:
                    div = div + dt
                elif c == 3:
                    div = div + (rp - rm)
                elif c == 4:
                    extra = {1: da, 2: dt, 3: rp - rm}
                partial.append(value)
            for c in range(5):
                if c == 0:
                    value = partial[0] - push_rho * div
                elif c == 4:
                    value = partial[4] - push_p * div
                else:
                    value = partial[c] - push_inv * extra[c]
                fbuf[new, c, row, t, pl.ds(r0 + PAD, CHUNK), :] = value
            return carry

        lax.fori_loop(0, radial // CHUNK, body, 0)
        if ghosted:
            ghosts(new, row, t)

    def patch(new, row, t, k):
        sign = 1.0 if row == 0 else -1.0
        half_u = scal_ref[row, 0] * (0.5 * sign * k)
        push_rho = scal_ref[row, 2] * (0.5 * sign * k)
        push_inv = scal_ref[row, 3] * (0.5 * sign * k)
        push_p = scal_ref[row, 4] * (0.5 * sign * k)
        here = is_last if row == 0 else is_first
        edge = width - 1 if row == 0 else 0

        def body(i, carry):
            r0 = pl.multiple_of(i * CHUNK, CHUNK)
            scale = eddy_ref[row, t - 1, pl.ds(r0, CHUNK), :] * k - half_u
            columns = gcol[pl.ds(r0, CHUNK), :]
            ghost = []
            for c in range(5):
                j = row * block + (t - 1) * 5 + c
                ghost.append(jnp.where(here, pltpu.roll(columns, (edge - j) % width, 1), 0.0))
            for c in range(5):
                delta = scale * ghost[c]
                if c == 0:
                    delta = delta - push_rho * ghost[1]
                elif c == 1:
                    delta = delta - push_inv * ghost[4]
                elif c == 4:
                    delta = delta - push_p * ghost[1]
                where = (new, c, row, t, pl.ds(r0 + PAD, CHUNK))
                fbuf[where] = fbuf[where] + delta
            return carry

        lax.fori_loop(0, radial // CHUNK, body, 0)
        ghosts(new, row, t)

    loads[0].wait()
    send_halo(0, 0)
    for row in range(2):
        pack(0, row, range(1, cells + 1), True)
        send_plane(0, row)
    for row in range(2):
        for t in range(cells):
            ghosts(0, row, t + 1)
    for load in loads[1:]:
        load.wait()

    def prepare(t, carry):
        for c in range(5):
            for row in range(2):
                fixed[c, row, t] = (0.5 / PHYS_STEP) * fixed[c, row, t] - (
                    2.0 / PHYS_STEP
                ) * base[c, row, t]
        return carry

    lax.fori_loop(0, cells, prepare, 0)

    def section(s, carry):
        slot = lax.rem(s, 2)
        new = 1 - slot
        k = jnp.where(
            lax.rem(s, SECTIONS) == SECTIONS - 1,
            jnp.float32(WEIGHT_LAST * PSEUDO_STEP),
            jnp.float32(WEIGHT_EARLY * PSEUDO_STEP),
        )

        @pl.when(jnp.logical_and(s > 0, lax.rem(s, SECTIONS) == 0))
        def _():
            def keep(t, carry):
                for c in range(5):
                    for row in range(2):
                        base[c, row, t] = fbuf[slot, c, row, t + 1, pl.ds(PAD, radial), :]
                return carry

            lax.fori_loop(0, cells, keep, 0)

        inner = range(2, cells)
        send_halo(slot, 1, (0,))
        for row in range(2):
            for t in inner:
                layer(slot, new, row, t, k, False)
        interface(slot)

        @pl.when(s > 0)
        def _():
            for row in range(2):
                for side in range(2):
                    halo_wait_send(new, row, side)

        for row in range(2):
            if row == 1:
                for t in inner:
                    patch(new, row, t, k)
                pack(new, row, inner, True)
            halo_wait_recv(slot, row, 1)
            if cells == 1:
                halo_wait_recv(slot, row, 0)
            layer(slot, new, row, 1, k, True)
            if cells > 1:
                halo_wait_recv(slot, row, 0)
                layer(slot, new, row, cells, k, True)
            if row == 0:

                @pl.when(s < total - 1)
                def _():
                    send_halo(new, 0, (0,))

                for t in inner:
                    patch(new, row, t, k)
                pack(new, row, inner, True)

            @pl.when(s < total - 1)
            def _():
                pack(new, row, sorted({1, cells}), False)
                send_plane(new, row)
                if row == 0:
                    send_halo(new, 0, (1,))

        return carry

    lax.fori_loop(0, total, section, 0)
    for row in range(2):
        for side in range(2):
            halo_wait_send((total - 1) % 2, row, side)
    store = pltpu.make_async_copy(
        fbuf.at[total % 2, :, :, pl.ds(1, cells), pl.ds(PAD, radial)], out_ref, load_sem.at[0]
    )
    store.start()
    store.wait()


def per_device(state_now, state_prev, eddy_visc, mean_flow, offset):
    _, _, cells, radial, width = state_now.shape
    count = lax.axis_size("theta")
    levels = exchange_levels(count)
    messages = exchange_messages(count)
    shift_cells = offset[0] % (cells * count)
    sectors = shift_cells // cells
    digits = jnp.stack(
        [sectors // stride % radix for stride, radix in levels] + [shift_cells % cells]
    ).astype(jnp.int32)
    scalars = jnp.stack(
        [
            mean_flow[:, 0],
            mean_flow[:, 1],
            mean_flow[:, 2],
            1.0 / mean_flow[:, 2],
            mean_flow[:, 2] * mean_flow[:, 3] * mean_flow[:, 3],
        ],
        axis=1,
    )
    block = -(-5 * cells // 8) * 8
    f32 = jnp.float32
    return pl.pallas_call(
        functools.partial(kernel, count, cells, radial),
        out_shape=jax.ShapeDtypeStruct(state_now.shape, f32),
        in_specs=[
            pl.BlockSpec(memory_space=pltpu.SMEM),
            pl.BlockSpec(memory_space=pltpu.SMEM),
            pl.BlockSpec(memory_space=pl.ANY),
            pl.BlockSpec(memory_space=pl.ANY),
            pl.BlockSpec(memory_space=pltpu.VMEM),
        ],
        out_specs=pl.BlockSpec(memory_space=pl.ANY),
        scratch_shapes=[
            pltpu.VMEM((2, 5, 2, cells + 2, radial + 2 * PAD, width), f32),
            pltpu.VMEM((5, 2, cells, radial, width), f32),
            pltpu.VMEM((5, 2, cells, radial, width), f32),
            pltpu.VMEM((radial, width), f32),
            pltpu.VMEM((2, radial, width), f32),
            pltpu.VMEM((2, len(levels), 2, block, radial), f32),
            pltpu.VMEM((2, len(messages), block, radial), f32),
            pltpu.SemaphoreType.DMA((3,)),
            pltpu.SemaphoreType.DMA((2, 2, 2, 2)),
            pltpu.SemaphoreType.DMA((2, 2, 2, 2)),
            pltpu.SemaphoreType.DMA((2, len(messages))),
            pltpu.SemaphoreType.DMA((2, len(messages))),
        ],
        compiler_params=pltpu.CompilerParams(
            collective_id=0, has_side_effects=True, vmem_limit_bytes=48 * 1024 * 1024
        ),
    )(scalars, digits, state_now, state_prev, eddy_visc)


def solution(mesh):
    placed = (
        P(None, None, "theta", "groups", None),
        P(None, None, "theta", "groups", None),
        P(None, "theta", "groups", None),
        P(),
        P("groups"),
    )
    return jax.shard_map(
        per_device,
        mesh=mesh,
        in_specs=placed,
        out_specs=P(None, None, "theta", "groups", None),
        check_vma=False,
    )
```

```python
import functools
import jax
import jax.numpy as jnp
from jax import lax
from jax.experimental import pallas as pl
from jax.experimental.pallas import tpu as pltpu
from jax.sharding import PartitionSpec as P

ITERS = 2
PSEUDO_STEP = 0.2
PHYS_STEP = 1.0
SECTIONS = 3
WEIGHT_EARLY = 0.6
WEIGHT_LAST = 1.0
PAD = 8
CHUNK = 64
FIRST = (3, 1)


def exchange_levels(count):
    levels = []
    stride = 1
    while stride < count:
        radix = 4 if (count // stride) % 4 == 0 else count // stride
        levels.append((stride, radix))
        stride *= radix
    return levels[::-1]


def exchange_messages(count):
    out = []
    for level, (stride, radix) in enumerate(exchange_levels(count)):
        top = radix if stride > 1 else radix + 1
        for j in range(1, top):
            for row in range(2):
                out.append((level, stride * j, row))
    return out


def kernel(
    count, cells, radial,
    scal_ref, digit_ref, now_ref, prev_ref, eddy_ref,
    out_ref,
    fbuf, base, fixed, gcol, packed, ifs, ifr, load_sem, hsend, hrecv, isend, irecv,
):
    me = lax.axis_index("theta")
    levels = exchange_levels(count)
    messages = exchange_messages(count)
    total = ITERS * SECTIONS
    width = fbuf.shape[-1]
    block = ifs.shape[-2]

    def peer(steps):
        return {"theta": lax.rem(me + (steps % count), count)}

    loads = [
        pltpu.make_async_copy(
            now_ref, fbuf.at[0, :, :, pl.ds(1, cells), pl.ds(PAD, radial)], load_sem.at[0]
        ),
        pltpu.make_async_copy(now_ref, base, load_sem.at[1]),
        pltpu.make_async_copy(prev_ref, fixed, load_sem.at[2]),
    ]
    for load in loads:
        load.start()

    reach = {1 % count, count - 1}
    for _, steps, _ in messages:
        reach |= {steps % count, -steps % count}
    reach = sorted(reach - {0})
    barrier = pltpu.get_barrier_semaphore()
    for steps in reach:
        pl.semaphore_signal(
            barrier, inc=1, device_id=peer(steps), device_id_type=pl.DeviceIdType.MESH
        )
    pl.semaphore_wait(barrier, len(reach))

    def halo(slot, row, side, piece=0):
        part = pl.ds(0, FIRST[row]) if piece == 0 else pl.ds(FIRST[row], 5 - FIRST[row])
        source, target = (1, cells + 1) if side == 0 else (cells, 0)
        return pltpu.make_async_remote_copy(
            src_ref=fbuf.at[slot, part, row, source, pl.ds(PAD, radial)],
            dst_ref=fbuf.at[slot, part, row, target, pl.ds(PAD, radial)],
            send_sem=hsend.at[slot, row, side, piece],
            recv_sem=hrecv.at[slot, row, side, piece],
            device_id=peer(-1 if side == 0 else 1),
            device_id_type=pl.DeviceIdType.MESH,
        )

    def plane_message(slot, index):
        level, steps, row = messages[index]
        return pltpu.make_async_remote_copy(
            src_ref=ifs.at[slot, level, row],
            dst_ref=ifr.at[slot, index],
            send_sem=isend.at[slot, index],
            recv_sem=irecv.at[slot, index],
            device_id=peer(steps if row == 0 else -steps),
            device_id_type=pl.DeviceIdType.MESH,
        )

    def of_level(level):
        return [index for index, message in enumerate(messages) if message[0] == level]

    def ghosts(slot, row, t):
        for c in range(5):
            sign = -1.0 if c == 3 else 1.0
            fbuf[slot, c, row, t, pl.ds(PAD - 1, 1), :] = (
                sign * fbuf[slot, c, row, t, pl.ds(PAD, 1), :]
            )
            fbuf[slot, c, row, t, pl.ds(PAD + radial, 1), :] = (
                sign * fbuf[slot, c, row, t, pl.ds(PAD + radial - 1, 1), :]
            )

    lane = lax.broadcasted_iota(jnp.int32, (radial, width), 1)

    def pack(slot, row, layers, fresh):
        acc = jnp.zeros((radial, width), jnp.float32) if fresh else packed[row]
        edge = width - 1 if row == 0 else 0
        for t in layers:
            for c in range(5):
                j = (t - 1) * 5 + c
                plane = fbuf[slot, c, row, t, pl.ds(PAD, radial), :]
                acc = jnp.where(lane == j, pltpu.roll(plane, (j - edge) % width, 1), acc)
        packed[row] = acc

    def send_plane(slot, row):
        ifs[slot, 0, row] = packed[row].T[:block]
        for index in of_level(0):
            if messages[index][2] == row:
                plane_message(slot, index).start()

    def send_halo(slot, row, pieces=(0, 1)):
        for piece in pieces:
            for side in range(2):
                halo(slot, row, side, piece).start()

    def halo_wait_send(slot, row, side):
        for piece in range(2):
            halo(slot, row, side, piece).wait_send()

    def halo_wait_recv(slot, row, side):
        for piece in range(2):
            halo(slot, row, side, piece).wait_recv()

    def pick(values, digit):
        out = values[0]
        for j in range(1, len(values)):
            out = jnp.where(digit == j, values[j], out)
        return out

    def interface(slot):
        near = far = None
        for level, (stride, radix) in enumerate(levels):
            got = ([ifs[slot, level, 0]], [ifs[slot, level, 1]])
            for index in of_level(level):
                plane_message(slot, index).wait()
            for index in of_level(level):
                got[messages[index][2]].append(ifr[slot, index])
            digit = digit_ref[level]
            near = [pick(got[row][:radix], digit) for row in range(2)]
            if stride > 1:
                for row in range(2):
                    ifs[slot, level + 1, row] = near[row]
                for index in of_level(level + 1):
                    plane_message(slot, index).start()
            if level == max(0, len(levels) - 2):
                send_halo(slot, 1, (1,))
            else:
                far = [pick(got[row][1 : radix + 1], digit) for row in range(2)]
        used = 5 * cells
        within = digit_ref[len(levels)]
        from_rotor = jnp.concatenate([far[0][:used], near[0][:used]], axis=0)
        from_stator = jnp.concatenate([near[1][:used], far[1][:used]], axis=0)
        low = pick(
            [from_rotor[5 * (cells - m) : 5 * (2 * cells - m)] for m in range(cells)], within
        )
        high = pick([from_stator[5 * m : 5 * (m + cells)] for m in range(cells)], within)
        gap = jnp.zeros((block - used, width), jnp.float32)
        rest = jnp.zeros((width - 2 * block, width), jnp.float32)
        gcol[...] = jnp.concatenate([high, gap, low, gap, rest], axis=0).T

    small = lax.broadcasted_iota(jnp.int32, (CHUNK, width), 1)
    is_first = small == 0
    is_last = small == width - 1

    def layer(slot, new, row, t, k, ghosted):
        half_u = scal_ref[row, 0] * (0.5 * k)
        half_v = scal_ref[row, 1] * (0.5 * k)
        push_rho = scal_ref[row, 2] * (0.5 * k)
        push_inv = scal_ref[row, 3] * (0.5 * k)
        push_p = scal_ref[row, 4] * (0.5 * k)

        def body(i, carry):
            r0 = pl.multiple_of(i * CHUNK, CHUNK)
            ke = eddy_ref[row, t - 1, pl.ds(r0, CHUNK), :] * k
            cf = ke * 6.0 + (1.5 / PHYS_STEP) * k
            columns = gcol[pl.ds(r0, CHUNK), :] if ghosted else None
            partial = []
            extra = {}
            div = None
            for c in range(5):
                f = fbuf[slot, c, row, t, pl.ds(r0 + PAD, CHUNK), :]
                rm = fbuf[slot, c, row, t, pl.ds(r0 + (PAD - 1), CHUNK), :]
                rp = fbuf[slot, c, row, t, pl.ds(r0 + (PAD + 1), CHUNK), :]
                tm = fbuf[slot, c, row, t - 1, pl.ds(r0 + PAD, CHUNK), :]
                tp = fbuf[slot, c, row, t + 1, pl.ds(r0 + PAD, CHUNK), :]
                am = pltpu.roll(f, 1, 1)
                ap = pltpu.roll(f, width - 1, 1)
                j = row * block + (t - 1) * 5 + c
                if row == 0:
                    am = jnp.where(is_first, 0.0, am)
                    ghost = pltpu.roll(columns, width - 1 - j, 1) if ghosted else 0.0
                    ap = jnp.where(is_last, ghost, ap)
                else:
                    ghost = pltpu.roll(columns, (width - j) % width, 1) if ghosted else 0.0
                    am = jnp.where(is_first, ghost, am)
                    ap = jnp.where(is_last, f, ap)
                da = ap - am
                dt = tp - tm
                around = (ap + am) + (tp + tm) + (rp + rm)
                value = (
                    base[c, row, t - 1, pl.ds(r0, CHUNK), :]
                    - k * fixed[c, row, t - 1, pl.ds(r0, CHUNK), :]
                    - cf * f
                    + ke * around
                    - half_u * da
                    - half_v * dt
                )
                if c == 1:
                    div = da
                elif c == 2:
                    div = div + dt
                elif c == 3:
                    div = div + (rp - rm)
                elif c == 4:
                    extra = {1: da, 2: dt, 3: rp - rm}
                partial.append(value)
            for c in range(5):
                if c == 0:
                    value = partial[0] - push_rho * div
                elif c == 4:
                    value = partial[4] - push_p * div
                else:
                    value = partial[c] - push_inv * extra[c]
                fbuf[new, c, row, t, pl.ds(r0 + PAD, CHUNK), :] = value
            return carry

        lax.fori_loop(0, radial // CHUNK, body, 0)
        if ghosted:
            ghosts(new, row, t)

    def patch(new, row, t, k):
        sign = 1.0 if row == 0 else -1.0
        half_u = scal_ref[row, 0] * (0.5 * sign * k)
        push_rho = scal_ref[row, 2] * (0.5 * sign * k)
        push_inv = scal_ref[row, 3] * (0.5 * sign * k)
        push_p = scal_ref[row, 4] * (0.5 * sign * k)
        here = is_last if row == 0 else is_first
        edge = width - 1 if row == 0 else 0

        def body(i, carry):
            r0 = pl.multiple_of(i * CHUNK, CHUNK)
            scale = eddy_ref[row, t - 1, pl.ds(r0, CHUNK), :] * k - half_u
            columns = gcol[pl.ds(r0, CHUNK), :]
            ghost = []
            for c in range(5):
                j = row * block + (t - 1) * 5 + c
                ghost.append(jnp.where(here, pltpu.roll(columns, (edge - j) % width, 1), 0.0))
            for c in range(5):
                delta = scale * ghost[c]
                if c == 0:
                    delta = delta - push_rho * ghost[1]
                elif c == 1:
                    delta = delta - push_inv * ghost[4]
                elif c == 4:
                    delta = delta - push_p * ghost[1]
                where = (new, c, row, t, pl.ds(r0 + PAD, CHUNK))
                fbuf[where] = fbuf[where] + delta
            return carry

        lax.fori_loop(0, radial // CHUNK, body, 0)
        ghosts(new, row, t)

    loads[0].wait()
    send_halo(0, 0)
    for row in range(2):
        pack(0, row, range(1, cells + 1), True)
        send_plane(0, row)
    for row in range(2):
        for t in range(cells):
            ghosts(0, row, t + 1)
    for load in loads[1:]:
        load.wait()

    def prepare(t, carry):
        for c in range(5):
            for row in range(2):
                fixed[c, row, t] = (0.5 / PHYS_STEP) * fixed[c, row, t] - (
                    2.0 / PHYS_STEP
                ) * base[c, row, t]
        return carry

    lax.fori_loop(0, cells, prepare, 0)

    def section(s, carry):
        slot = lax.rem(s, 2)
        new = 1 - slot
        k = jnp.where(
            lax.rem(s, SECTIONS) == SECTIONS - 1,
            jnp.float32(WEIGHT_LAST * PSEUDO_STEP),
            jnp.float32(WEIGHT_EARLY * PSEUDO_STEP),
        )

        @pl.when(jnp.logical_and(s > 0, lax.rem(s, SECTIONS) == 0))
        def _():
            def keep(t, carry):
                for c in range(5):
                    for row in range(2):
                        base[c, row, t] = fbuf[slot, c, row, t + 1, pl.ds(PAD, radial), :]
                return carry

            lax.fori_loop(0, cells, keep, 0)

        inner = range(2, cells)
        send_halo(slot, 1, (0,))
        for row in range(2):
            for t in inner:
                layer(slot, new, row, t, k, False)
        interface(slot)

        @pl.when(s > 0)
        def _():
            for row in range(2):
                for side in range(2):
                    halo_wait_send(new, row, side)

        for row in range(2):
            if row == 1:
                for t in inner:
                    patch(new, row, t, k)
                pack(new, row, inner, True)
            halo_wait_recv(slot, row, 1)
            if cells == 1:
                halo_wait_recv(slot, row, 0)
            layer(slot, new, row, 1, k, True)
            if cells > 1:
                halo_wait_recv(slot, row, 0)
                layer(slot, new, row, cells, k, True)
            if row == 0:

                @pl.when(s < total - 1)
                def _():
                    send_halo(new, 0, (0,))

                for t in inner:
                    patch(new, row, t, k)
                pack(new, row, inner, True)

            @pl.when(s < total - 1)
            def _():
                pack(new, row, sorted({1, cells}), False)
                send_plane(new, row)
                if row == 0:
                    send_halo(new, 0, (1,))

        return carry

    lax.fori_loop(0, total, section, 0)
    for row in range(2):
        for side in range(2):
            halo_wait_send((total - 1) % 2, row, side)
    store = pltpu.make_async_copy(
        fbuf.at[total % 2, :, :, pl.ds(1, cells), pl.ds(PAD, radial)], out_ref, load_sem.at[0]
    )
    store.start()
    store.wait()


def per_device(state_now, state_prev, eddy_visc, mean_flow, offset):
    _, _, cells, radial, width = state_now.shape
    count = lax.axis_size("theta")
    levels = exchange_levels(count)
    messages = exchange_messages(count)
    shift_cells = offset[0] % (cells * count)
    sectors = shift_cells // cells
    digits = jnp.stack(
        [sectors // stride % radix for stride, radix in levels] + [shift_cells % cells]
    ).astype(jnp.int32)
    scalars = jnp.stack(
        [
            mean_flow[:, 0],
            mean_flow[:, 1],
            mean_flow[:, 2],
            1.0 / mean_flow[:, 2],
            mean_flow[:, 2] * mean_flow[:, 3] * mean_flow[:, 3],
        ],
        axis=1,
    )
    block = -(-5 * cells // 8) * 8
    f32 = jnp.float32
    return pl.pallas_call(
        functools.partial(kernel, count, cells, radial),
        out_shape=jax.ShapeDtypeStruct(state_now.shape, f32),
        in_specs=[
            pl.BlockSpec(memory_space=pltpu.SMEM),
            pl.BlockSpec(memory_space=pltpu.SMEM),
            pl.BlockSpec(memory_space=pl.ANY),
            pl.BlockSpec(memory_space=pl.ANY),
            pl.BlockSpec(memory_space=pltpu.VMEM),
        ],
        out_specs=pl.BlockSpec(memory_space=pl.ANY),
        scratch_shapes=[
            pltpu.VMEM((2, 5, 2, cells + 2, radial + 2 * PAD, width), f32),
            pltpu.VMEM((5, 2, cells, radial, width), f32),
            pltpu.VMEM((5, 2, cells, radial, width), f32),
            pltpu.VMEM((radial, width), f32),
            pltpu.VMEM((2, radial, width), f32),
            pltpu.VMEM((2, len(levels), 2, block, radial), f32),
            pltpu.VMEM((2, len(messages), block, radial), f32),
            pltpu.SemaphoreType.DMA((3,)),
            pltpu.SemaphoreType.DMA((2, 2, 2, 2)),
            pltpu.SemaphoreType.DMA((2, 2, 2, 2)),
            pltpu.SemaphoreType.DMA((2, len(messages))),
            pltpu.SemaphoreType.DMA((2, len(messages))),
        ],
        compiler_params=pltpu.CompilerParams(
            collective_id=0, has_side_effects=True, vmem_limit_bytes=48 * 1024 * 1024
        ),
    )(scalars, digits, state_now, state_prev, eddy_visc)


def solution(mesh):
    placed = (
        P(None, None, "theta", "groups", None),
        P(None, None, "theta", "groups", None),
        P(None, "theta", "groups", None),
        P(),
        P("groups"),
    )
    return jax.shard_map(
        per_device,
        mesh=mesh,
        in_specs=placed,
        out_specs=P(None, None, "theta", "groups", None),
        check_vma=False,
    )
```
